32 devices in a mesh: grp: 4 (over z), cp: 8 (over y, x, core).
Axes of the slice: x: 2, y: 2, z: 4, core: 2. Of those that a mesh axis runs over, the one named last changes fastest.
Arguments:
- query_states: bfloat16 [32, 256, 1024], P(('grp', 'cp')), may hold values from -130 to 130
- key_states: bfloat16 [32, 256, 128], P(('grp', 'cp')), may hold values from -8 to 8
- value_states: bfloat16 [32, 256, 128], P(('grp', 'cp')), may hold values from -6 to 6
- grad_output: bfloat16 [32, 256, 1024], P(('grp', 'cp')), may hold values from -6 to 6
- pair_kinds: int32 [16, 7], replicated, may hold values from 0 to 3, as said below
- row_start: int32 [2048], replicated, may hold values from 0 to 2046, as said below
Outputs:
- attn_out: bfloat16 [32, 256, 1024], P(('grp', 'cp'))
- grad_query: bfloat16 [32, 256, 1024], P(('grp', 'cp'))
- grad_key: bfloat16 [32, 256, 128], P(('grp', 'cp'))
- grad_value: bfloat16 [32, 256, 128], P(('grp', 'cp'))
The draws below stay inside these ranges and needn't reach their ends.
Inputs may be any that keep to these rules, and one draw needn't show every extreme that they name: `pair_kinds`: kinds are 0 to 3 as in the reference program; column 0 is 1 or 2; [b, d] is 3 wherever b - d < 0. row_start[t] lies between max(t - 768, 0) and max(t - 1, 0).
All inputs are finite; a program needn't handle non-finite values.
Results may differ from the reference program's by a relative error of at most 0.035.
Values may be sent and summed in bfloat16 or wider, within the bound.
No kernel may reach another device: no remote copies, remote signals or barrier semaphores. Data moves between devices by JAX's collectives and lax.ppermute only.
A program may use at most 64 MiB of HBM per device.

```python
from functools import partial
import jax
import jax.numpy as jnp
from jax import lax

KVH = 4
HD = 128
BLK = 128
REACH = 6
GQ = 8
OWNERS = 8
ROWS_DEV = 256
NB = 16
TOKENS = 2048


def shared_fields(key):
    folded = jax.random.fold_in(key, 11)
    draw_one, draw_two = jax.random.split(folded, 2)
    queries = jnp.clip(jax.random.normal(draw_one, (OWNERS * KVH, ROWS_DEV, GQ, HD), jnp.float32), -6.0, 6.0)
    states = jnp.clip(jax.random.normal(draw_two, (OWNERS * KVH, ROWS_DEV, HD), jnp.float32), -6.0, 6.0)
    return (queries, states)


def draw_query_states(key, part):
    queries, states = shared_fields(key)
    return queries.reshape(OWNERS * KVH, ROWS_DEV, GQ * HD).astype(jnp.bfloat16)


def draw_key_states(key, part):
    queries, states = shared_fields(key)
    return states.astype(jnp.bfloat16)


def draw_pair_kinds(key, part):
    folded = jax.random.fold_in(key, 23)
    draw_one, draw_two, draw_three, draw_four = jax.random.split(folded, 4)
    density = jax.random.randint(draw_one, (NB, 1), 0, REACH + 1)
    ranking = jax.random.randint(draw_two, (NB, REACH), 0, REACH)
    full_or_bounded = jax.random.randint(draw_three, (NB, REACH), 0, 2) * 2
    distant = jnp.where(ranking < density, full_or_bounded, 3)
    block_ids = jnp.arange(NB, dtype=jnp.int32)[:, None]
    distance = jnp.arange(1, REACH + 1, dtype=jnp.int32)[None, :]
    distant = jnp.where(block_ids - distance >= 0, distant, 3)
    diagonal = 1 + jax.random.randint(draw_four, (NB, 1), 0, 2)
    return jnp.concatenate([diagonal, distant], axis=1).astype(jnp.int32)


def draw_row_start(key, part):
    reach_rows = jax.random.randint(jax.random.fold_in(key, 31), (TOKENS,), 1, REACH * BLK + 1)
    return jnp.maximum(jnp.arange(TOKENS, dtype=jnp.int32) - reach_rows, 0).astype(jnp.int32)


def levels(stream_key, dims, cuts, least, high):
    level = 1.0
    for axis_at, parts in cuts:
        heights = jax.random.uniform(jax.random.fold_in(jax.random.fold_in(stream_key, 6), axis_at), (parts,), jnp.float32, least / len(cuts), high / len(cuts))
        level = level * jnp.repeat(jnp.exp(heights), dims[axis_at] // parts).reshape((-1,) + (1,) * (len(dims) - 1 - axis_at))
    return level


def normal_values(stream_key, extent, scale, bound, shards=(), kind=jnp.bfloat16):
    result = jax.random.normal(stream_key, extent, jnp.float32) * scale
    if len(shards) > 0:
        result = levels(stream_key, extent, shards, -0.22, 0.18) * result
    return jnp.clip(result, min=-bound, max=bound).astype(kind)


def setup_inputs(seed: int = 0) -> dict:
    streams_of = jax.random.split(jax.random.key(seed), 7)
    query_states = draw_query_states(jax.random.fold_in(streams_of[6], 71), 0)
    key_states = draw_key_states(jax.random.fold_in(streams_of[6], 71), 0)
    value_states = normal_values(streams_of[2], (OWNERS * KVH, ROWS_DEV, HD), 1.0, 6.0, ((0, 32),))
    grad_output = normal_values(streams_of[3], (OWNERS * KVH, ROWS_DEV, GQ * HD), 1.0, 6.0, ((0, 32),))
    pair_kinds = draw_pair_kinds(jax.random.fold_in(streams_of[6], 71), 0)
    row_start = draw_row_start(jax.random.fold_in(streams_of[6], 71), 0)
    return {"query_states": query_states, "key_states": key_states, "value_states": value_states, "grad_output": grad_output, "pair_kinds": pair_kinds, "row_start": row_start}


def window_mask(kinds_block, starts_block, row_first):
    window_width = (REACH + 1) * BLK
    query_pos = row_first + jnp.arange(BLK, dtype=jnp.int32)
    key_pos = row_first - REACH * BLK + jnp.arange(window_width, dtype=jnp.int32)
    kind_cols = jnp.repeat(kinds_block[::-1], BLK)
    before = key_pos[None, :] <= query_pos[:, None]
    inside = before & (key_pos[None, :] >= starts_block[:, None])
    return (kind_cols == 0)[None, :] | ((kind_cols == 1)[None, :] & before) | ((kind_cols == 2)[None, :] & inside)


def head_pass(fields, pair_kinds, row_start):
    head_queries, head_keys, head_values, head_grads = fields
    front_pad = REACH * BLK
    window_width = (REACH + 1) * BLK
    score_scale = HD ** -0.5
    padded_keys = jnp.concatenate([jnp.zeros((front_pad, HD), head_keys.dtype), head_keys], axis=0)
    padded_values = jnp.concatenate([jnp.zeros((front_pad, HD), head_values.dtype), head_values], axis=0)

    def advance(state, block_number):
        grad_keys, grad_values = state
        row_first = block_number * BLK
        query_block = lax.dynamic_slice_in_dim(head_queries, row_first, BLK, 0).astype(jnp.float32)
        grad_block = lax.dynamic_slice_in_dim(head_grads, row_first, BLK, 0).astype(jnp.float32)
        key_window = lax.dynamic_slice_in_dim(padded_keys, row_first, window_width, 0).astype(jnp.float32)
        value_window = lax.dynamic_slice_in_dim(padded_values, row_first, window_width, 0).astype(jnp.float32)
        kinds_block = lax.dynamic_slice_in_dim(pair_kinds, block_number, 1, 0)[0]
        starts_block = lax.dynamic_slice_in_dim(row_start, row_first, BLK, 0)
        allowed = window_mask(kinds_block, starts_block, row_first)
        scores = jnp.einsum("qgd,wd->gqw", query_block, key_window) * score_scale
        scores = jnp.where(allowed[None], scores, -jnp.inf)
        row_max = jnp.max(scores, axis=-1, keepdims=True)
        log_total = row_max + jnp.log(jnp.sum(jnp.exp(scores - row_max), axis=-1, keepdims=True))
        prob_full = jnp.exp(scores - log_total)
        prob_half = lax.optimization_barrier(prob_full.astype(jnp.bfloat16)).astype(jnp.float32)
        block_out = jnp.einsum("gqw,wd->qgd", prob_half, value_window).astype(jnp.bfloat16)
        out_wide = lax.optimization_barrier(block_out).astype(jnp.float32)
        row_dot = jnp.sum(grad_block * out_wide, axis=-1).T[:, :, None]
        prob_grad = jnp.einsum("qgd,wd->gqw", grad_block, value_window)
        score_grad = lax.optimization_barrier((prob_full * (prob_grad - row_dot)).astype(jnp.bfloat16)).astype(jnp.float32)
        query_grad = (jnp.einsum("gqw,wd->qgd", score_grad, key_window) * score_scale).astype(jnp.bfloat16)
        key_part = jnp.einsum("gqw,qgd->wd", score_grad, query_block) * score_scale
        value_part = jnp.einsum("gqw,qgd->wd", prob_half, grad_block)
        grad_keys = lax.dynamic_update_slice_in_dim(grad_keys, lax.dynamic_slice_in_dim(grad_keys, row_first, window_width, 0) + key_part, row_first, 0)
        grad_values = lax.dynamic_update_slice_in_dim(grad_values, lax.dynamic_slice_in_dim(grad_values, row_first, window_width, 0) + value_part, row_first, 0)
        return (grad_keys, grad_values), (block_out, query_grad)

    initial = (jnp.zeros((TOKENS + front_pad, HD), jnp.float32), jnp.zeros((TOKENS + front_pad, HD), jnp.float32))
    (grad_keys, grad_values), (block_outs, query_grads) = lax.scan(advance, initial, jnp.arange(TOKENS // BLK, dtype=jnp.int32))
    return (block_outs.reshape(TOKENS, GQ * HD), query_grads.reshape(TOKENS, GQ * HD), grad_keys[front_pad:].astype(jnp.bfloat16), grad_values[front_pad:].astype(jnp.bfloat16))


def by_head(array, trailing):
    return array.reshape((OWNERS, KVH, ROWS_DEV) + trailing).swapaxes(0, 1).reshape((KVH, TOKENS) + trailing)


def to_slots(array):
    return array.reshape(KVH, OWNERS, ROWS_DEV, -1).swapaxes(0, 1).reshape(OWNERS * KVH, ROWS_DEV, -1)


def reference(query_states, key_states, value_states, grad_output, pair_kinds, row_start):
    heads = (by_head(query_states, (GQ, HD)), by_head(key_states, (HD,)), by_head(value_states, (HD,)), by_head(grad_output, (GQ, HD)))
    attn_all, qgrad_all, kgrad_all, vgrad_all = lax.map(partial(head_pass, pair_kinds=pair_kinds, row_start=row_start), heads)
    return (to_slots(attn_all), to_slots(qgrad_all), to_slots(kgrad_all), to_slots(vgrad_all))
```

```python
import functools
import math

import jax
import jax.numpy as jnp
from jax import lax
from jax.experimental import pallas as pl
from jax.experimental.pallas import tpu as pltpu
from jax.sharding import PartitionSpec as P

KVH = 4
BLK = 128
REACH = 6
AXES = ("grp", "cp")
LOG2E = math.log2(math.e)
NT = (((1,), (1,)), ((), ()))
NN = (((1,), (0,)), ((), ()))
TN = (((0,), (0,)), ((), ()))


def dot(a, b, dims):
    return lax.dot_general(a, b, dims, preferred_element_type=jnp.float32)


def rotated(x, by):
    count = lax.axis_size(AXES[0]) * lax.axis_size(AXES[1])
    return lax.ppermute(x, AXES, [(i, (i + by) % count) for i in range(count)])


def fold(x, op):
    tall = x.reshape(x.shape[0] // 8, 8, x.shape[1])
    return op(tall, axis=0)


def kernel(kinds, starts, q, do, k, v, near, mid, far, o, dq, parts, own, kext, vext, pt, dst, st, dot_t):
    rows = q.shape[0]
    hd = k.shape[1]
    heads = q.shape[1] // hd
    nblk = rows // BLK
    win = (REACH + 1) * BLK
    scale = hd ** -0.5
    for n, part in enumerate((far, mid, near)):
        kext[n * rows : (n + 1) * rows, :] = part[0]
        vext[n * rows : (n + 1) * rows, :] = part[1]
    kext[3 * rows :, :] = k[...]
    vext[3 * rows :, :] = v[...]
    pair = 2
    width = pair * BLK
    acc = []
    for i in range(nblk):
        row = slice(i * BLK, (i + 1) * BLK)
        low = i * BLK
        start = starts[:, row]
        start2 = jnp.concatenate([start] * pair, axis=1)
        token = lax.broadcasted_iota(jnp.int32, (1, BLK), 1)
        token2 = jnp.concatenate([token] * pair, axis=1)
        key_at = lax.broadcasted_iota(jnp.int32, (BLK, width), 0)
        bounds = []
        for j in range(REACH + 1):
            d = REACH - j
            kind = kinds[i * (REACH + 1) + d]
            lo = jnp.where(kind == 2, start2 - kinds[nblk * (REACH + 1)] - (i - d) * BLK, -1)
            bounds.append(jnp.where(kind == 3, BLK, lo))
        for hp in range(heads // pair):
            cols = slice(hp * width, (hp + 1) * width)
            q2 = jnp.concatenate(
                [q[row, h * hd : (h + 1) * hd] for h in range(hp * pair, (hp + 1) * pair)], axis=0
            )
            d2 = jnp.concatenate(
                [do[row, h * hd : (h + 1) * hd].T for h in range(hp * pair, (hp + 1) * pair)], axis=1
            ).astype(jnp.float32)
            top = None
            for j in range(REACH + 1):
                keys = slice(j * BLK, (j + 1) * BLK)
                s = dot(kext[low + j * BLK : low + (j + 1) * BLK, :], q2, NT)
                ok = key_at >= bounds[j]
                if j == REACH:
                    ok = ok & (key_at <= token2)
                s = jnp.where(ok, s, -jnp.inf)
                st[keys, :] = s
                part = fold(s, jnp.max)
                top = part if top is None else jnp.maximum(top, part)
            top = jnp.max(top, axis=0, keepdims=True) * (scale * LOG2E)
            total = None
            for j in range(REACH + 1):
                keys = slice(j * BLK, (j + 1) * BLK)
                p = jnp.exp2(st[keys, :] * (scale * LOG2E) - top)
                part = fold(p, jnp.sum)
                total = part if total is None else total + part
                pt[keys, cols] = p.astype(jnp.bfloat16)
            inv = 1.0 / jnp.sum(total, axis=0, keepdims=True)
            ot = dot(vext[low : low + win, :], pt[:, cols], TN) * inv
            for h in range(pair):
                o[row, (hp * pair + h) * hd : (hp * pair + h + 1) * hd] = ot[:, h * BLK : (h + 1) * BLK].T.astype(jnp.bfloat16)
            d2 = d2 * inv
            rd = jnp.sum(d2 * ot.astype(jnp.bfloat16).astype(jnp.float32), axis=0, keepdims=True)
            d2 = d2.astype(jnp.bfloat16)
            dot_t[:, cols] = d2
            for j in range(REACH + 1):
                keys = slice(j * BLK, (j + 1) * BLK)
                dp = dot(vext[low + j * BLK : low + (j + 1) * BLK, :], d2, NN)
                dst[keys, cols] = (pt[keys, cols].astype(jnp.float32) * (dp - rd)).astype(jnp.bfloat16)
            dqt = dot(kext[low : low + win, :], dst[:, cols], TN) * scale
            for h in range(pair):
                dq[row, (hp * pair + h) * hd : (hp * pair + h + 1) * hd] = dqt[:, h * BLK : (h + 1) * BLK].T.astype(jnp.bfloat16)
        qall = jnp.concatenate([q[row, h * hd : (h + 1) * hd] for h in range(heads)], axis=0)
        dk_w = dot(dst[...], qall, NN) * scale
        dv_w = dot(pt[...], dot_t[...], NT)
        acc.append((dk_w, dv_w))
    for n in range(4 * nblk):
        for t in range(2):
            total = None
            for i in range(nblk):
                if 0 <= n - i <= REACH:
                    piece = acc[i][t][(n - i) * BLK : (n - i + 1) * BLK]
                    total = piece if total is None else total + piece
            b, at = divmod(n, nblk)
            if b == 3:
                own[t, at * BLK : (at + 1) * BLK, :] = total
            else:
                parts[b, t, at * BLK : (at + 1) * BLK, :] = total.astype(jnp.bfloat16)


def local(query_states, key_states, value_states, grad_output, pair_kinds, row_start):
    rows = query_states.shape[1]
    hd = key_states.shape[2]
    width = query_states.shape[2]
    nblk = rows // BLK
    win = (REACH + 1) * BLK
    owner = lax.axis_index(AXES) // KVH
    kv = jnp.concatenate([key_states, value_states], axis=0)
    mid = rotated(kv, 2 * KVH)
    near = rotated(kv, KVH)
    far = rotated(mid, KVH)
    kinds = lax.dynamic_slice_in_dim(pair_kinds, owner * nblk, nblk, 0).reshape(-1)
    kinds = jnp.concatenate([kinds, (owner * rows)[None].astype(jnp.int32)])
    starts = lax.dynamic_slice_in_dim(row_start, owner * rows, rows, 0).reshape(1, rows)
    vm = pl.BlockSpec(memory_space=pltpu.VMEM)
    o, dq, parts, own = pl.pallas_call(
        kernel,
        out_shape=(
            jax.ShapeDtypeStruct((rows, width), jnp.bfloat16),
            jax.ShapeDtypeStruct((rows, width), jnp.bfloat16),
            jax.ShapeDtypeStruct((3, 2, rows, hd), jnp.bfloat16),
            jax.ShapeDtypeStruct((2, rows, hd), jnp.float32),
        ),
        in_specs=[pl.BlockSpec(memory_space=pltpu.SMEM)] + [vm] * 8,
        out_specs=(vm, vm, vm, vm),
        scratch_shapes=[
            pltpu.VMEM((4 * rows, hd), jnp.bfloat16),
            pltpu.VMEM((4 * rows, hd), jnp.bfloat16),
            pltpu.VMEM((win, width), jnp.bfloat16),
            pltpu.VMEM((win, width), jnp.bfloat16),
            pltpu.VMEM((win, 2 * BLK), jnp.float32),
            pltpu.VMEM((hd, width), jnp.bfloat16),
        ],
        compiler_params=pltpu.CompilerParams(vmem_limit_bytes=32 << 20),
        cost_estimate=pl.CostEstimate(flops=12 * rows * width * win, bytes_accessed=3 << 20, transcendentals=rows * win * 8),
        name="attention",
    )(kinds, starts, query_states[0], grad_output[0], key_states[0], value_states[0], near, mid, far)
    back = rotated(parts[0], -KVH)
    direct = rotated(parts[2], -KVH)
    summed = (parts[1].astype(jnp.float32) + back.astype(jnp.float32)).astype(jnp.bfloat16)
    twice = rotated(summed, -2 * KVH)
    grads = (own + direct.astype(jnp.float32) + twice.astype(jnp.float32)).astype(jnp.bfloat16)
    return (o[None], dq[None], grads[0][None], grads[1][None])


def solution(mesh):
    placed = (P(AXES, None, None),) * 4 + (P(), P())
    return jax.shard_map(
        local, mesh=mesh, in_specs=placed, out_specs=(P(AXES, None, None),) * 4, check_vma=False
    )
```

```python
import functools
import math

import jax
import jax.numpy as jnp
from jax import lax
from jax.experimental import pallas as pl
from jax.experimental.pallas import tpu as pltpu
from jax.sharding import PartitionSpec as P

KVH = 4
BLK = 128
REACH = 6
COLS = REACH + 1
AXES = ("grp", "cp")
LOG2E = math.log2(math.e)
WIDE = 2 * BLK
ONES = 16
HALF, SINGLE = jnp.bfloat16, jnp.float32
NT = (((1,), (1,)), ((), ()))
NN = (((1,), (0,)), ((), ()))


def dot(a, b, dims=NN):
    return lax.dot_general(a, b, dims, preferred_element_type=SINGLE)


def rotated(x, by):
    count = lax.axis_size(AXES[0]) * lax.axis_size(AXES[1])
    return lax.ppermute(x, AXES, [(i, (i + by) % count) for i in range(count)])


def folded(x, op):
    return op(x.reshape(x.shape[0] // 8, 8, x.shape[1]), axis=0)


def two(x):
    return jnp.concatenate([x, x], axis=1)


def block(n):
    return slice(n * BLK, (n + 1) * BLK)


def groups(ref):
    return [slice(c, c + WIDE) for c in range(0, ref.shape[-1], WIDE)]


def with_ones(vals_t):
    return jnp.concatenate([vals_t, jnp.ones((ONES, vals_t.shape[1]), HALF)], axis=0)


def lower_bound(kind, start2, base):
    lo = jnp.where(kind == 2, start2 - base, -1)
    return jnp.where(kind == 3, BLK, lo)


def forward_item(i, qt, keys, vals, bounds, diagonal, before, after, keep_p, keep_m):
    hd = qt.shape[1]
    scale = hd ** -0.5 * LOG2E
    cuts = groups(qt)
    ahead = dot(keys, qt[i, :, cuts[0]])
    for g, cols in enumerate(cuts):
        s = ahead
        if g + 1 < len(cuts):
            ahead = dot(keys, qt[i, :, cuts[g + 1]])
        parts = []
        key_at = lax.broadcasted_iota(jnp.int32, (BLK, WIDE), 0)
        for n, lo in enumerate(bounds):
            ok = key_at >= lo
            if diagonal == n:
                ok = ok & (key_at <= two(lax.broadcasted_iota(jnp.int32, (1, BLK), 1)))
            parts.append(jnp.where(ok, s[block(n)], -jnp.inf))
        top = functools.reduce(jnp.maximum, [folded(x, jnp.max) for x in parts])
        top = jnp.max(top, axis=0, keepdims=True) * scale
        if before is not None:
            old = before[0][i, :, cols]
            top = jnp.maximum(old, top)
        p = jnp.concatenate([jnp.exp2(x * scale - top).astype(HALF) for x in parts], axis=0)
        keep_p(cols, p)
        keep_m(cols, top)
        out = dot(vals, p)
        total, out = out[hd : hd + 1], out[:hd]
        if before is not None:
            fade = jnp.exp2(old - top)
            total = total + before[1][i, :, cols] * fade
            out = out + before[2][i, :, cols] * fade
        after[0][i, :, cols] = top
        after[1][i, :, cols] = total
        after[2][i, :, cols] = out


def backward_item(i, qt, dt, keys_t, vals, p, fac, rd, dq_add, dk_add, dv_add, ds_s, dt_s):
    depth = vals.shape[0]
    cuts = groups(qt)
    rd = rd * fac

    def scaled(cols):
        x = (dt[i, :, cols].astype(SINGLE) * fac[:, cols]).astype(HALF)
        dt_s[:, cols] = x
        return dot(vals, x)

    ahead = scaled(cuts[0])
    for g, cols in enumerate(cuts):
        dp = ahead
        if g + 1 < len(cuts):
            ahead = scaled(cuts[g + 1])
        ds = (dp - rd[:, cols]).astype(HALF) * p[:, cols]
        ds_s[0:depth, cols] = ds
        dq_add(cols, dot(keys_t, ds))
    dk_add(dot(qt[i], ds_s[0:depth, :], NT))
    dv_add(dot(dt_s[...], p[...], NT))


def stack_kernel(k, v, kv, sems):
    copies = [pltpu.make_async_copy(x, kv.at[n], sems.at[n]) for n, x in enumerate((k, v))]
    for copy in copies:
        copy.start()
    for copy in copies:
        copy.wait()


def own_blocks(i):
    return list(range(i, -1, -1))


def prep_kernel(kinds, starts, q_hbm, do_hbm, kv, qt, dt, own_p, own_m, top_m, total, acc, q, do, sems):
    rows, width = q.shape
    hd = kv.shape[2]
    nblk = rows // BLK
    heads = width // hd
    copies = [pltpu.make_async_copy(q_hbm, q, sems.at[0]), pltpu.make_async_copy(do_hbm, do, sems.at[1])]
    for copy in copies:
        copy.start()
    for copy, source, turned in ((copies[0], q, qt), (copies[1], do, dt)):
        copy.wait()
        for i in range(nblk):
            for h in range(heads):
                turned[i, :, block(h)] = source[block(i), h * hd : (h + 1) * hd].T
    for i in range(nblk):
        start2 = two(starts[:, block(i)])
        names = own_blocks(i)
        depth = len(names) * BLK
        bounds = [
            lower_bound(kinds[i * COLS + i - n], start2, kinds[nblk * COLS] + n * BLK) for n in names
        ]
        keys = jnp.concatenate([kv[0, block(n)] for n in names], axis=0)
        vals = jnp.concatenate([kv[1, block(n)].T for n in names], axis=1)

        def keep_p(cols, x, i=i, depth=depth):
            own_p[i, 0:depth, cols] = x

        def keep_m(cols, x, i=i):
            own_m[i, :, cols] = x

        forward_item(i, qt, keys, with_ones(vals), bounds, 0, None, (top_m, total, acc), keep_p, keep_m)


def listed(kinds, names, sorts, i):
    count = jnp.int32(0)
    for n in range(REACH - 1, 1, -1):
        kind = kinds[i * COLS + REACH + i - n]
        names[i, count] = n
        sorts[i, count] = kind
        count = count + jnp.where(kind == 3, 0, 1)
    names[i, count] = REACH - 1
    sorts[i, count] = 3
    return (count + 1) // 2


def near_kernel(kinds, starts, qt, near, mid, top_in, total_in, acc_in, kt, vx, phat, ref_m, top_m, total, acc, kx, vt, names, sorts):
    hd = qt.shape[1]
    nblk = qt.shape[0]
    steps = nblk
    for n in range(nblk):
        for b, kv in enumerate((mid, near)):
            slot = nblk * b + n
            kx[slot] = kv[0, block(n)]
            vx[slot] = kv[1, block(n)]
            kt[slot] = kv[0, block(n)].T
            vt[slot] = kv[1, block(n)].T
    counts = [listed(kinds, names, sorts, i) for i in range(nblk)]
    top_m[...] = top_in[...]
    total[...] = total_in[...]
    acc[...] = acc_in[...]
    for i in range(nblk):
        start2 = two(starts[:, block(i)])

        @pl.loop(0, counts[i])
        def _(step, i=i, start2=start2):
            blocks = [names[i, 2 * step + n] for n in range(2)]
            bounds = [
                lower_bound(sorts[i, 2 * step + n], start2, kinds[nblk * COLS] + (blocks[n] - REACH) * BLK)
                for n in range(2)
            ]
            keys = jnp.concatenate([kx[b - 2] for b in blocks], axis=0)
            vals = jnp.concatenate([vt[b - 2] for b in blocks], axis=1)
            state = (top_m, total, acc)

            def keep_p(cols, x):
                phat[i * steps + step, :, cols] = x

            def keep_m(cols, x):
                ref_m[i * steps + step, :, cols] = x

            forward_item(i, qt, keys, with_ones(vals), bounds, None, state, state, keep_p, keep_m)


def far_kernel(kinds, starts, qt, dt, far, top_m, total, acc, part, out_t, fin_m, inv_l, rd, dq, far_p, fin_l, out_s, grads, ds_s, dt_s):
    hd = qt.shape[1]
    nblk = qt.shape[0]
    grads[...] = jnp.zeros_like(grads)
    lives = []
    for i in range(nblk):
        start2 = two(starts[:, block(i)])
        at = slice(i * BLK, 2 * BLK)
        depth = (2 - i) * BLK
        live = kinds[i * COLS + REACH] != 3
        for n in range(i + 1, 2):
            live = live | (kinds[i * COLS + REACH + i - n] != 3)
        lives.append(live)

        @pl.when(live)
        def _(i=i, start2=start2, at=at, depth=depth):
            bounds = [
                lower_bound(kinds[i * COLS + REACH + i - n], start2, kinds[nblk * COLS] + (n - REACH) * BLK)
                for n in range(i, 2)
            ]

            def keep_p(cols, x):
                far_p[i, 0:depth, cols] = x

            forward_item(
                i, qt, far[0, at], with_ones(far[1, at].T), bounds, None, (top_m, total, acc),
                (fin_m, fin_l, out_s), keep_p, lambda cols, x: None,
            )

        @pl.when(jnp.logical_not(live))
        def _(i=i):
            fin_m[i] = top_m[i]
            fin_l[i] = total[i]
            out_s[i] = acc[i]
            dq[i] = jnp.zeros(dq.shape[1:], dq.dtype)

    for i in range(nblk):
        for cols in groups(qt):
            inv = 1.0 / fin_l[i, :, cols]
            inv_l[i, :, cols] = inv
            out = (out_s[i, :, cols] * inv).astype(HALF)
            out_t[i, :, cols] = out
            prod = out.astype(SINGLE) * dt[i, :, cols].astype(SINGLE)
            rd[i, :, cols] = jnp.sum(folded(prod, jnp.sum), axis=0, keepdims=True)

    for i in range(nblk):
        at = slice(i * BLK, 2 * BLK)
        depth = (2 - i) * BLK

        @pl.when(lives[i])
        def _(i=i, at=at, depth=depth):
            def dq_add(cols, x):
                dq[i, :, cols] = x

            def adder(t):
                def add(x):
                    grads[t, :, at] = grads[t, :, at] + x

                return add

            backward_item(
                i, qt, dt, far[0, at].T, far[1, at], far_p.at[i, 0:depth], inv_l[i], rd[i], dq_add, adder(0), adder(1),
                ds_s, dt_s,
            )

    for t, factor in enumerate((hd ** -0.5, 1.0)):
        for n in range(2):
            part[t, block(n)] = (grads[t, :, block(n)] * factor).T.astype(HALF)


def rest_kernel(kinds, qt, dt, kt, vx, phat, ref_m, fin_m, inv_l, rd, dq_in, mid, near, dq, grads, names, sorts, ds_s, dt_s):
    hd = qt.shape[1]
    nblk = qt.shape[0]
    steps = nblk
    counts = [listed(kinds, names, sorts, i) for i in range(nblk)]
    grads[...] = jnp.zeros_like(grads)
    dq[...] = dq_in[...]
    for i in range(nblk):

        @pl.loop(0, counts[i])
        def _(step, i=i):
            blocks = [names[i, 2 * step + n] - 2 for n in range(2)]
            fac = jnp.exp2(ref_m[i * steps + step] - fin_m[i]) * inv_l[i]
            keys_t = jnp.concatenate([kt[b] for b in blocks], axis=1)
            vals = jnp.concatenate([vx[b] for b in blocks], axis=0)

            def dq_add(cols, x):
                dq[i, :, cols] = dq[i, :, cols] + x

            def adder(t):
                def add(x):
                    for n in range(2):
                        grads[t, blocks[n]] = grads[t, blocks[n]] + x[:, block(n)]

                return add

            backward_item(
                i, qt, dt, keys_t, vals, phat.at[i * steps + step], fac, rd[i], dq_add, adder(0), adder(1), ds_s, dt_s
            )

    for t, factor in enumerate((hd ** -0.5, 1.0)):
        for n in range(nblk):
            mid[t, block(n)] = (grads[t, n] * factor).T
            near[t, block(n)] = (grads[t, nblk + n] * factor).T.astype(HALF)


def last_kernel(qt, dt, kv, own_p, own_m, fin_m, inv_l, rd, dq_in, out_t, own, o, dq, dq_s, grads, ds_s, dt_s):
    hd = qt.shape[1]
    nblk = qt.shape[0]
    heads = qt.shape[2] // BLK
    for i in range(nblk):
        names = own_blocks(i)
        depth = len(names) * BLK
        fac = jnp.exp2(own_m[i] - fin_m[i]) * inv_l[i]
        keys_t = jnp.concatenate([kv[0, block(n)].T for n in names], axis=1)
        vals = jnp.concatenate([kv[1, block(n)] for n in names], axis=0)

        def dq_add(cols, x, i=i):
            dq_s[i, :, cols] = dq_in[i, :, cols] + x

        def adder(t, names=names, i=i):
            def add(x):
                for at, n in enumerate(names):
                    piece = x[:, block(at)]
                    grads[t, n] = piece if n == i else grads[t, n] + piece

            return add

        backward_item(
            i, qt, dt, keys_t, vals, own_p.at[i, 0:depth], fac, rd[i], dq_add, adder(0), adder(1), ds_s, dt_s
        )
    for t, factor in enumerate((hd ** -0.5, 1.0)):
        for n in range(nblk):
            own[t, block(n)] = (grads[t, n] * factor).T
    for i in range(nblk):
        for h in range(heads):
            o[block(i), h * hd : (h + 1) * hd] = out_t[i, :, block(h)].T
            dq[block(i), h * hd : (h + 1) * hd] = (dq_s[i, :, block(h)] * hd ** -0.5).astype(HALF).T


def local(query_states, key_states, value_states, grad_output, pair_kinds, row_start):
    rows = query_states.shape[1]
    hd = key_states.shape[2]
    width = query_states.shape[2]
    nblk = rows // BLK
    lanes = width // hd * BLK
    slots = 2 * nblk
    owner = lax.axis_index(AXES) // KVH
    vm = pl.BlockSpec(memory_space=pltpu.VMEM)
    sm = pl.BlockSpec(memory_space=pltpu.SMEM)
    hbm = pl.BlockSpec(memory_space=pltpu.HBM)

    def call(body, name, specs, outs, scratch, units, *args):
        return pl.pallas_call(
            body,
            out_shape=tuple(jax.ShapeDtypeStruct(s, t) for s, t in outs),
            in_specs=specs,
            out_specs=tuple(vm for _ in outs),
            scratch_shapes=scratch,
            compiler_params=pltpu.CompilerParams(vmem_limit_bytes=16 << 20),
            cost_estimate=pl.CostEstimate(
                flops=units * 4 * BLK * BLK * lanes, bytes_accessed=1 << 19, transcendentals=0
            ),
            name=name,
        )(*args)

    (kv,) = call(
        stack_kernel, "stack", [hbm, hbm], [((2, rows, hd), HALF)], [pltpu.SemaphoreType.DMA((2,))], 1,
        pltpu.with_memory_space_constraint(key_states[0], pltpu.HBM),
        pltpu.with_memory_space_constraint(value_states[0], pltpu.HBM),
    )
    mid = rotated(kv, 2 * KVH)
    near = rotated(kv, KVH)
    kinds = lax.dynamic_slice_in_dim(pair_kinds, owner * nblk, nblk, 0).reshape(-1)
    kinds = jnp.concatenate([kinds, (owner * rows)[None].astype(jnp.int32)])
    starts = lax.dynamic_slice_in_dim(row_start, owner * rows, rows, 0).reshape(1, rows)
    rows_t = ((nblk, hd, lanes), HALF)
    wide_t = ((nblk, hd, lanes), SINGLE)
    stat = ((nblk, 1, lanes), SINGLE)
    probs = ((nblk, 2 * BLK, lanes), HALF)
    lists = [pltpu.SMEM((nblk, 8), jnp.int32)] * 2
    stage = [pltpu.VMEM((2 * BLK, lanes), HALF), pltpu.VMEM((hd, lanes), HALF)]
    qt, dt, own_p, own_m, top_m, total, acc = call(
        prep_kernel, "prep", [sm, vm, hbm, hbm, vm], [rows_t, rows_t, probs, stat, stat, stat, wide_t],
        [pltpu.VMEM((rows, width), HALF)] * 2 + [pltpu.SemaphoreType.DMA((2,))], 20,
        kinds, starts, pltpu.with_memory_space_constraint(query_states[0], pltpu.HBM),
        pltpu.with_memory_space_constraint(grad_output[0], pltpu.HBM), kv,
    )
    mid, qt = lax.optimization_barrier((mid, qt))
    far = rotated(mid, KVH)
    tile = ((slots, BLK, hd), HALF)
    kt, vx, phat, ref_m, top_m, total, acc = call(
        near_kernel, "near", [sm] + [vm] * 7,
        [tile, tile, ((nblk * nblk, 2 * BLK, lanes), HALF), ((nblk * nblk, 1, lanes), SINGLE), stat, stat, wide_t],
        [pltpu.VMEM(*tile), pltpu.VMEM(*tile)] + lists, 20,
        kinds, starts, qt, near, mid, top_m, total, acc,
    )
    far_part, out_t, fin_m, inv_l, rd, dq_t = call(
        far_kernel, "far", [sm] + [vm] * 7, [((2, rows, hd), HALF), rows_t, stat, stat, stat, wide_t],
        [pltpu.VMEM(*probs), pltpu.VMEM(*stat), pltpu.VMEM(*wide_t), pltpu.VMEM((2, hd, rows), SINGLE)] + stage, 20,
        kinds, starts, qt, dt, far, top_m, total, acc,
    )
    back = rotated(far_part, -KVH)
    mid_part, near_part, dq_t = call(
        rest_kernel, "rest", [sm] + [vm] * 10,
        [((2, rows, hd), SINGLE), ((2, rows, hd), HALF), wide_t],
        [pltpu.VMEM((2, slots, hd, BLK), SINGLE)] + lists + stage, 20,
        kinds, qt, dt, kt, vx, phat, ref_m, fin_m, inv_l, rd, dq_t,
    )
    direct = rotated(near_part, -KVH)
    twice = rotated((mid_part + back.astype(SINGLE)).astype(HALF), -2 * KVH)
    own, o, dq = call(
        last_kernel, "last", [vm] * 10, [((2, rows, hd), SINGLE), ((rows, width), HALF), ((rows, width), HALF)],
        [pltpu.VMEM(*wide_t), pltpu.VMEM((2, nblk, hd, BLK), SINGLE)] + stage, 20,
        qt, dt, kv, own_p, own_m, fin_m, inv_l, rd, dq_t, out_t,
    )
    grads = (own + direct.astype(SINGLE) + twice.astype(SINGLE)).astype(HALF)
    return (o[None], dq[None], grads[0][None], grads[1][None])


def solution(mesh):
    placed = (P(AXES, None, None),) * 4 + (P(), P())
    return jax.shard_map(
        local, mesh=mesh, in_specs=placed, out_specs=(P(AXES, None, None),) * 4, check_vma=False
    )
```
